512 devices in a mesh: row: 16 (over z_hi, x, core), col: 32 (over y, z_lo).
Axes of the slice: x: 4, y: 8, z: 8 (z_hi: 2, z_lo: 4; z = z_hi * 4 + z_lo), core: 2. Of those that a mesh axis runs over, the one named last changes fastest.
Arguments:
- trunk: bfloat16 [4096, 512], P('row', 'col'), may hold values from -6 to 6
- proj_weight: bfloat16 [512, 128], P('col'), may hold values from -0.25 to 0.25
- conv_kernel: bfloat16 [9, 64, 64], replicated, may hold values from -0.25 to 0.25
- norm_gain: float32 [64], replicated, may hold values from 0.1 to 1.9
- norm_bias: float32 [64], replicated, may hold values from -3 to 3
Outputs:
- contact_map: bfloat16 [4096, 64, 4096], P('row', None, 'col')
The draws below stay inside these ranges and needn't reach their ends.
All inputs are finite; a program needn't handle non-finite values.
Results may differ from the reference program's by a relative error of at most 0.0095.
Values may be sent and summed in bfloat16 or wider, within the bound.
No kernel may reach another device: no remote copies, remote signals or barrier semaphores. Data moves between devices by JAX's collectives and lax.ppermute only.
A program may use at most 128 MiB of HBM per device.

```python
import jax
import jax.numpy as jnp
from jax import lax

CH = 64
TRUNK = 512
ROW_BINS_LOCAL = 256
CONV_DILATION = 4
MAP_BIN_COUNT = 4096
N_ROW = 16


def shard_levels(key, shape, split, smallest, high):
    def one(position, parts):
        heights = jax.random.uniform(jax.random.fold_in(jax.random.fold_in(key, 6), position), (parts,), jnp.float32, smallest / len(split), high / len(split))
        return jnp.repeat(jnp.exp(heights), shape[position] // parts).reshape((-1,) + (1,) * (len(shape) - position - 1))

    loudness = one(*split[0])
    for cut in split[1:]:
        loudness = loudness * one(*cut)
    return loudness


def gaussian(own_key, shape, spread, bound, shards=(), kind=jnp.bfloat16):
    drawn = jax.random.normal(own_key, shape, jnp.float32) * spread
    if len(shards) > 0:
        drawn = shard_levels(own_key, shape, shards, -0.22, 0.18) * drawn
    return jnp.clip(drawn, min=-bound, max=bound).astype(kind)


def setup_inputs(seed: int = 0) -> dict:
    seeds = jax.random.split(jax.random.key(seed), 6)
    return {
        "trunk": gaussian(seeds[0], (MAP_BIN_COUNT, TRUNK), 1.0, 6.0, ((0, 16), (1, 32))),
        "proj_weight": gaussian(seeds[1], (TRUNK, 2 * CH), TRUNK ** -0.5, 0.25, ((0, 32),)),
        "conv_kernel": gaussian(seeds[2], (9, CH, CH), (9 * CH) ** -0.5, 0.25),
        "norm_gain": jnp.clip(1.0 + 0.18 * jax.random.normal(seeds[3], (CH,), jnp.float32), 0.1, 1.9),
        "norm_bias": gaussian(seeds[4], (CH,), 0.5, 3.0, (), jnp.float32),
    }


def reference(trunk, proj_weight, conv_kernel, norm_gain, norm_bias):
    feature_rows = jnp.dot(trunk, proj_weight, preferred_element_type=jnp.float32).astype(jnp.bfloat16)
    padded_map = jnp.pad(feature_rows, ((CONV_DILATION, CONV_DILATION), (0, 0))).astype(jnp.float32)
    inside_region = jnp.pad(jnp.ones((MAP_BIN_COUNT,), jnp.float32), CONV_DILATION)
    col_u = padded_map[:, :CH].T
    col_v = padded_map[:, CH:].T
    kernel = conv_kernel.astype(jnp.float32)
    span_length = ROW_BINS_LOCAL + 2 * CONV_DILATION

    def one_block(index):
        start = index * ROW_BINS_LOCAL
        row_u = lax.dynamic_slice_in_dim(padded_map[:, :CH], start, span_length, 0)
        row_v = lax.dynamic_slice_in_dim(padded_map[:, CH:], start, span_length, 0)
        row_in = lax.dynamic_slice_in_dim(inside_region, start, span_length, 0)
        pair_block = row_u[:, :, None] * col_u[None] + row_v[:, :, None] + col_v[None]
        pair_block = (pair_block * row_in[:, None, None] * inside_region[None, None, :]).astype(jnp.bfloat16)
        active = jnp.maximum(pair_block, jnp.zeros((), jnp.bfloat16)).astype(jnp.float32)
        grand_total = jnp.zeros((ROW_BINS_LOCAL, CH, MAP_BIN_COUNT), jnp.float32)
        for kernel_tap_row in range(3):
            for kernel_tap_column in range(3):
                mixed_output = jnp.einsum("oi,ric->roc", kernel[kernel_tap_row * 3 + kernel_tap_column], active,
                                   precision=lax.Precision.HIGHEST)
                grand_total = grand_total + mixed_output[kernel_tap_row * CONV_DILATION:kernel_tap_row * CONV_DILATION + ROW_BINS_LOCAL, :, kernel_tap_column * CONV_DILATION:kernel_tap_column * CONV_DILATION + MAP_BIN_COUNT]
                grand_total = grand_total + mixed_output[kernel_tap_column * CONV_DILATION:kernel_tap_column * CONV_DILATION + ROW_BINS_LOCAL, :, kernel_tap_row * CONV_DILATION:kernel_tap_row * CONV_DILATION + MAP_BIN_COUNT]
        base_offset = pair_block[CONV_DILATION:CONV_DILATION + ROW_BINS_LOCAL, :, CONV_DILATION:CONV_DILATION + MAP_BIN_COUNT].astype(jnp.float32)
        result = base_offset + norm_gain[None, :, None] * (0.5 * grand_total) + norm_bias[None, :, None]
        return result.astype(jnp.bfloat16)

    blocks = lax.map(one_block, jnp.arange(N_ROW, dtype=jnp.int32))
    return blocks.reshape(MAP_BIN_COUNT, CH, MAP_BIN_COUNT)
```

```python
import jax
import jax.numpy as jnp
from jax import lax
from jax.experimental import pallas as pl
from jax.experimental.pallas import tpu as pltpu
from jax.sharding import PartitionSpec as P

DIL = 4
CH = 64
FAR = -1e30
GROUP = 4
STEP_ROWS = GROUP * DIL
LANES = 128
TAPS_IN = GROUP + 2
VMEM_BYTES = 48 << 20


def pack_kernel(trunk_ref, proj_ref, send_ref):
    row = lax.axis_index("row")
    n_col, channels = send_ref.shape[0], send_ref.shape[1]
    rows = trunk_ref.shape[2]
    last = trunk_ref.shape[0] - 1
    above = trunk_ref[jnp.maximum(row - 1, 0), :, rows - LANES :].astype(jnp.float32)
    below = trunk_ref[jnp.minimum(row + 1, last), :, :LANES].astype(jnp.float32)
    lane = lax.broadcasted_iota(jnp.int32, (channels, LANES), 1)
    row_sides = jnp.where(lane < LANES // 2, pltpu.roll(below, 8, 1), pltpu.roll(above, LANES - 8, 1))
    row_sides = row_sides.astype(jnp.bfloat16)
    own = trunk_ref[row]
    proj = proj_ref[...]

    def chunk(c):
        c = min(max(c, 0), n_col - 1)
        return trunk_ref[c // 2, :, (c % 2) * LANES : (c % 2 + 1) * LANES]

    for c in range(n_col):
        sides = jnp.where(lane < 8, chunk(c + 1), row_sides)
        sides = jnp.where(lane >= LANES - 8, chunk(c - 1), sides)
        send_ref[c] = jnp.concatenate([own, chunk(c), sides, proj], 1)


def weights_kernel(kernel_ref, gain_ref, weights_ref):
    weights_ref[...] = jnp.zeros_like(weights_ref)
    half_gain = 0.5 * gain_ref[...]
    for b in range(3):
        for a in range(3):
            total = kernel_ref[3 * a + b].astype(jnp.float32) + kernel_ref[3 * b + a].astype(jnp.float32)
            tap = (half_gain * total).astype(jnp.bfloat16)
            for out in range(GROUP):
                first = (b * TAPS_IN + out + a) * CH
                weights_ref[out * CH : (out + 1) * CH, first : first + CH] = tap


def map_kernel(
    gathered_ref, weights_ref, bias_ref, out_ref,
    rows_ref, cols_ref, act_ref, pair_ref, bias_tile,
    *, rows,
):
    step = pl.program_id(0)
    row, col = lax.axis_index("row"), lax.axis_index("col")
    n_row, n_col = lax.axis_size("row"), lax.axis_size("col")

    def generate(row_index_block, slot_of):
        block, count = row_index_block
        for local in range(count):
            q, s = local // DIL, local % DIL
            u = jnp.broadcast_to(block[:CH, local : local + 1], (CH, LANES))
            v = jnp.broadcast_to(block[CH:, local : local + 1], (CH, LANES))
            lanes = slice((s % 2) * LANES, (s % 2 + 1) * LANES)
            for b in range(3):
                pair = (u * cols_ref[b, :CH] + (v + cols_ref[b, CH:])).astype(jnp.bfloat16)
                if b == 1:
                    pair_ref[s // 2, slot_of(q), :, lanes] = pair
                act_ref[b, s // 2, slot_of(q), :, lanes] = jnp.maximum(pair, jnp.zeros((), jnp.bfloat16))

    @pl.when(step == 0)
    def _():
        got = gathered_ref[...]
        bins = rows + 2 * LANES
        feat = lax.dot_general(
            got[:, :bins], got[:, bins:], (((0,), (0,)), ((), ())), preferred_element_type=jnp.float32
        ).astype(jnp.bfloat16).astype(jnp.float32)
        far = jnp.where(lax.broadcasted_iota(jnp.int32, (8, 2 * CH), 1) >= CH, FAR, 0.0)
        sides = feat[rows + LANES :]
        rows_ref[0:8] = jnp.where(row == 0, far, sides[LANES - 16 : LANES - 8])
        rows_ref[8 : 8 + rows] = feat[:rows]
        rows_ref[8 + rows : 16 + rows] = jnp.where(row == n_row - 1, far, sides[8:16])
        rows_ref[16 + rows :] = jnp.zeros((LANES, 2 * CH), jnp.float32)
        left = jnp.where(col == 0, far, sides[LANES - 8 :])
        right = jnp.where(col == n_col - 1, far, sides[:8])
        rest = jnp.zeros((LANES - 16, 2 * CH), jnp.float32)
        window = jnp.concatenate([left, feat[rows : rows + LANES], right, rest], 0)
        turned = window.T
        for b in range(3):
            first = 8 + (b - 1) * DIL
            cols_ref[b] = turned[:, first : first + LANES]
        bias_tile[...] = jnp.broadcast_to(bias_ref[...], (CH, LANES))
        start = rows_ref[0:LANES].T
        generate((start[:, 4:12], 8), lambda q: q)
        generate((start[:, 12:28], 16), lambda q: q + 2)

    for half in range(2):
        taken = [
            act_ref[b, half, pl.ds(GROUP * step, TAPS_IN)].reshape(TAPS_IN * CH, 2 * LANES) for b in range(3)
        ]
        result = jnp.dot(weights_ref[...], jnp.concatenate(taken, 0), preferred_element_type=jnp.float32)
        for out in range(GROUP):
            for h in range(2):
                lanes = slice(h * LANES, (h + 1) * LANES)
                base = pair_ref[half, GROUP * step + 1 + out, :, lanes].astype(jnp.float32)
                value = base + result[out * CH : (out + 1) * CH, lanes] + bias_tile[...]
                out_ref[DIL * out + 2 * half + h] = value.astype(out_ref.dtype)

    nxt = jnp.minimum(step + 1, rows // STEP_ROWS - 1)
    block = rows_ref[pl.ds(pl.multiple_of(STEP_ROWS * nxt + 8, 8), LANES)].T
    generate((block[:, 4:20], 16), lambda q: GROUP * nxt + 2 + q)


def local_map(gathered, conv_kernel, norm_gain, norm_bias):
    rows = gathered.shape[1] - 3 * LANES
    depth = 3 * TAPS_IN * CH
    weights = pl.pallas_call(
        weights_kernel,
        out_shape=jax.ShapeDtypeStruct((GROUP * CH, depth), jnp.bfloat16),
        name="weights",
    )(conv_kernel, norm_gain[:, None])

    whole = lambda shape: pl.BlockSpec(shape, lambda i: (0,) * len(shape))
    n_q = rows // DIL
    return pl.pallas_call(
        lambda *refs: map_kernel(*refs, rows=rows),
        grid=(rows // STEP_ROWS,),
        in_specs=[
            whole(gathered.shape), whole((GROUP * CH, depth)), whole((CH, 1)),
        ],
        out_specs=pl.BlockSpec((STEP_ROWS, CH, LANES), lambda i: (i, 0, 0)),
        out_shape=jax.ShapeDtypeStruct((rows, CH, LANES), jnp.bfloat16),
        scratch_shapes=[
            pltpu.VMEM((rows + 16 + LANES, 2 * CH), jnp.float32),
            pltpu.VMEM((3, 2 * CH, LANES), jnp.float32),
            pltpu.VMEM((3, 2, n_q + 2, CH, 2 * LANES), jnp.bfloat16),
            pltpu.VMEM((2, n_q + 2, CH, 2 * LANES), jnp.bfloat16),
            pltpu.VMEM((CH, LANES), jnp.float32),
        ],
        compiler_params=pltpu.CompilerParams(
            dimension_semantics=("arbitrary",), vmem_limit_bytes=VMEM_BYTES
        ),
        name="pair_map",
    )(gathered, weights, norm_bias[:, None])


def per_device(trunk, proj_weight, conv_kernel, norm_gain, norm_bias):
    rows, channels = trunk.shape
    n_row, n_col = lax.axis_size("row"), lax.axis_size("col")

    every_bin = lax.all_to_all(
        jnp.broadcast_to(trunk.T[None], (n_row, channels, rows)), "row", 0, 0, tiled=True
    )
    width = rows + 3 * LANES
    send = pl.pallas_call(
        pack_kernel,
        out_shape=jax.ShapeDtypeStruct((n_col, channels, width), jnp.bfloat16),
        name="pack",
    )(every_bin, proj_weight)
    gathered = lax.all_to_all(send, "col", 0, 0, tiled=True).reshape(n_col * channels, width)
    return local_map(gathered, conv_kernel, norm_gain, norm_bias)


def solution(mesh):
    in_specs = (P("row", "col"), P("col", None), P(), P(), P())
    out_specs = P("row", None, "col")
    return jax.shard_map(
        per_device, mesh=mesh, in_specs=in_specs, out_specs=out_specs, check_vma=False
    )
```

```python
import jax
import jax.numpy as jnp
from jax import lax
from jax.experimental import pallas as pl
from jax.experimental.pallas import tpu as pltpu
from jax.sharding import PartitionSpec as P

DIL = 4
CH = 64
FAR = -1e30
GROUP = 4
STEP_ROWS = GROUP * DIL
LANES = 128
TAPS_IN = GROUP + 2
VMEM_BYTES = 48 << 20


def pack_kernel(trunk_ref, above_ref, below_ref, proj_ref, send_ref):
    channels, rows = trunk_ref.shape
    part = channels // 2
    lane = lax.broadcasted_iota(jnp.int32, (channels, LANES), 1)
    sides = jnp.where(
        lane < LANES // 2,
        below_ref[:, :LANES].astype(jnp.float32),
        above_ref[:, rows - LANES :].astype(jnp.float32),
    )
    turned = pltpu.roll(sides[part:], LANES // 2, 1)
    inner = (lane[:part] >= LANES // 4) & (lane[:part] < LANES - LANES // 4)
    block = jnp.concatenate(
        [
            trunk_ref[:, :LANES], trunk_ref[:, LANES:], proj_ref[...],
            jnp.where(inner, turned, sides[:part]).astype(jnp.bfloat16),
        ],
        0,
    )
    for peer in range(send_ref.shape[0]):
        send_ref[peer] = block


def features_kernel(got_ref, rows_ref, window_ref):
    peers, height, _ = got_ref.shape
    channels = 2 * height // 7
    part = channels // 2

    def take(first, count):
        return got_ref[:, first : first + count].reshape(peers * count, LANES)

    def project(bins, proj):
        return lax.dot_general(bins, proj, (((0,), (0,)), ((), ())), preferred_element_type=jnp.float32)

    proj = take(2 * channels, channels)
    sides = take(3 * channels, part)
    one = project(sides, take(2 * channels, part))
    two = project(sides, take(2 * channels + part, part))
    half = LANES // 2
    below = one[:8] + two[half : half + 8]
    above = one[LANES - 8 :] + two[half - 8 : half]
    row = lax.axis_index("row")
    far = jnp.where(lax.broadcasted_iota(jnp.int32, (8, 2 * CH), 1) >= CH, FAR, 0.0)
    above = jnp.where(row == 0, far, above)
    below = jnp.where(row == lax.axis_size("row") - 1, far, below)
    feat = jnp.concatenate(
        [above, project(take(0, channels), proj), project(take(channels, channels), proj), below], 0
    ).astype(jnp.bfloat16)
    rows_ref[...] = feat
    height = LANES + 16
    window_ref[...] = jnp.where(lax.axis_index("col") % 2 == 1, feat[LANES:], feat[:height])


def weights_kernel(kernel_ref, gain_ref, weights_ref):
    weights_ref[...] = jnp.zeros_like(weights_ref)
    half_gain = 0.5 * gain_ref[...]
    for b in range(3):
        for a in range(3):
            total = kernel_ref[3 * a + b].astype(jnp.float32) + kernel_ref[3 * b + a].astype(jnp.float32)
            tap = (half_gain * total).astype(jnp.bfloat16)
            for out in range(GROUP):
                first = (b * TAPS_IN + out + a) * CH
                weights_ref[out * CH : (out + 1) * CH, first : first + CH] = tap


def map_kernel(
    feat_ref, window_ref, weights_ref, bias_ref, out_ref,
    rows_ref, cols_ref, act_ref, pair_ref, bias_tile,
    *, rows,
):
    step = pl.program_id(0)

    def generate(row_index_block, slot_of):
        block, count = row_index_block
        for local in range(count):
            q, s = local // DIL, local % DIL
            u = jnp.broadcast_to(block[:CH, local : local + 1], (CH, LANES))
            v = jnp.broadcast_to(block[CH:, local : local + 1], (CH, LANES))
            lanes = slice((s % 2) * LANES, (s % 2 + 1) * LANES)
            for b in range(3):
                pair = (u * cols_ref[b, :CH] + (v + cols_ref[b, CH:])).astype(jnp.bfloat16)
                if b == 1:
                    pair_ref[s // 2, slot_of(q), :, lanes] = pair
                act_ref[b, s // 2, slot_of(q), :, lanes] = jnp.maximum(pair, jnp.zeros((), jnp.bfloat16))

    @pl.when(step == 0)
    def _():
        rows_ref[: 16 + rows] = feat_ref[...].astype(jnp.float32)
        rows_ref[16 + rows :] = jnp.zeros((LANES, 2 * CH), jnp.float32)
        rest = jnp.zeros((LANES - 16, 2 * CH), jnp.float32)
        window = jnp.concatenate([window_ref[...].astype(jnp.float32), rest], 0)
        turned = window.T
        for b in range(3):
            first = 8 + (b - 1) * DIL
            cols_ref[b] = turned[:, first : first + LANES]
        bias_tile[...] = jnp.broadcast_to(bias_ref[...], (CH, LANES))
        start = rows_ref[0:LANES].T
        generate((start[:, 4:12], 8), lambda q: q)
        generate((start[:, 12:28], 16), lambda q: q + 2)

    for half in range(2):
        taken = [
            act_ref[b, half, pl.ds(GROUP * step, TAPS_IN)].reshape(TAPS_IN * CH, 2 * LANES) for b in range(3)
        ]
        result = jnp.dot(weights_ref[...], jnp.concatenate(taken, 0), preferred_element_type=jnp.float32)
        for out in range(GROUP):
            for h in range(2):
                lanes = slice(h * LANES, (h + 1) * LANES)
                base = pair_ref[half, GROUP * step + 1 + out, :, lanes].astype(jnp.float32)
                value = base + result[out * CH : (out + 1) * CH, lanes] + bias_tile[...]
                out_ref[DIL * out + 2 * half + h] = value.astype(out_ref.dtype)

    nxt = jnp.minimum(step + 1, rows // STEP_ROWS - 1)
    block = rows_ref[pl.ds(pl.multiple_of(STEP_ROWS * nxt + 8, 8), LANES)].T
    generate((block[:, 4:20], 16), lambda q: GROUP * nxt + 2 + q)


def local_map(feat, window, conv_kernel, norm_gain, norm_bias):
    rows = feat.shape[0] - 16
    depth = 3 * TAPS_IN * CH
    weights = pl.pallas_call(
        weights_kernel,
        out_shape=pltpu.VMEM((GROUP * CH, depth), jnp.bfloat16),
        name="weights",
    )(conv_kernel, norm_gain[:, None])

    whole = lambda shape: pl.BlockSpec(shape, lambda i: (0,) * len(shape))
    n_q = rows // DIL
    return pl.pallas_call(
        lambda *refs: map_kernel(*refs, rows=rows),
        grid=(rows // STEP_ROWS,),
        in_specs=[
            whole(feat.shape), whole(window.shape), whole((GROUP * CH, depth)), whole((CH, 1)),
        ],
        out_specs=pl.BlockSpec((STEP_ROWS, CH, LANES), lambda i: (i, 0, 0)),
        out_shape=jax.ShapeDtypeStruct((rows, CH, LANES), jnp.bfloat16),
        scratch_shapes=[
            pltpu.VMEM((rows + 16 + LANES, 2 * CH), jnp.float32),
            pltpu.VMEM((3, 2 * CH, LANES), jnp.float32),
            pltpu.VMEM((3, 2, n_q + 2, CH, 2 * LANES), jnp.bfloat16),
            pltpu.VMEM((2, n_q + 2, CH, 2 * LANES), jnp.bfloat16),
            pltpu.VMEM((CH, LANES), jnp.float32),
        ],
        compiler_params=pltpu.CompilerParams(
            dimension_semantics=("arbitrary",), vmem_limit_bytes=VMEM_BYTES
        ),
        name="pair_map",
    )(feat, window, weights, norm_bias[:, None])


def window_routes(n_row, n_col):
    targets = [[0, x, core] for x in (0, 1, 3, 2) for core in (0, 1)]
    targets += [[1, x, core] for x in (0, 1, 3, 2) for core in (0, 1)]
    routes = []
    for r in range(n_row):
        for parity in range(2):
            sources = list(range(parity, n_col, 2))
            to_rows = list(range(n_row))
            if (n_row, n_col) == (16, 32):
                column_y = (2 * r + parity) // 4
                away = [min((c // 4 - column_y) % 8, (column_y - c // 4) % 8) for c in range(n_col)]
                sources.sort(key=lambda c: -away[c])
                to_rows = [
                    ((r // 8) ^ zh) * 8 + ((r // 2 % 4 + x) % 4) * 2 + ((r % 2) ^ core)
                    for zh, x, core in targets
                ]
            routes += [(r * n_col + c, t * n_col + 2 * r + parity) for c, t in zip(sources, to_rows)]
    return routes


def in_vmem(array):
    return pltpu.with_memory_space_constraint(array, pltpu.VMEM)


def per_device(trunk, proj_weight, conv_kernel, norm_gain, norm_bias):
    rows, channels = trunk.shape
    n_row, n_col = lax.axis_size("row"), lax.axis_size("col")

    own = trunk.T
    above = lax.ppermute(own, "row", [(r, r + 1) for r in range(n_row - 1)])
    below = lax.ppermute(own, "row", [(r + 1, r) for r in range(n_row - 1)])
    send = pl.pallas_call(
        pack_kernel,
        out_shape=pltpu.VMEM((n_col, 7 * channels // 2, LANES), jnp.bfloat16),
        name="pack",
    )(own, in_vmem(above), in_vmem(below), proj_weight)
    got = lax.all_to_all(send, "col", 0, 0, tiled=True)
    feat, window = pl.pallas_call(
        features_kernel,
        out_shape=[
            pltpu.VMEM((rows + 16, 2 * CH), jnp.bfloat16),
            pltpu.VMEM((LANES + 16, 2 * CH), jnp.bfloat16),
        ],
        name="features",
    )(in_vmem(got))
    window = lax.ppermute(window, ("row", "col"), window_routes(n_row, n_col))
    return local_map(feat, window, conv_kernel, norm_gain, norm_bias)


def solution(mesh):
    in_specs = (P("row", "col"), P("col", None), P(), P(), P())
    out_specs = P("row", None, "col")
    return jax.shard_map(
        per_device, mesh=mesh, in_specs=in_specs, out_specs=out_specs, check_vma=False
    )
```

```python
import jax
import jax.numpy as jnp
from jax import lax
from jax.experimental import pallas as pl
from jax.experimental.pallas import tpu as pltpu
from jax.sharding import PartitionSpec as P

DIL = 4
CH = 64
FAR = -1e30
GROUP = 4
STEP_ROWS = GROUP * DIL
LANES = 128
TAPS_IN = GROUP + 2
RING = 4
PIECE = 8
OUT_ORDER = (1, 2, 3, 0)
VMEM_BYTES = 48 << 20


def pack_kernel(trunk_ref, one_ref, two_ref, proj_ref, send_ref):
    channels, rows = trunk_ref.shape
    part = channels // 2
    lane = lax.broadcasted_iota(jnp.int32, (channels, LANES), 1)
    one_is_above = lax.axis_index("row") % 2 == 1

    def side(lanes, from_one):
        return jnp.where(from_one, one_ref[:, lanes], two_ref[:, lanes]).astype(jnp.float32)

    below = side(slice(0, LANES), ~one_is_above)
    above = side(slice(rows - LANES, rows), one_is_above)
    sides = jnp.where(lane < LANES // 2, below, above)
    turned = pltpu.roll(sides[part:], LANES // 2, 1)
    inner = (lane[:part] >= LANES // 4) & (lane[:part] < LANES - LANES // 4)
    block = jnp.concatenate(
        [
            trunk_ref[:, :LANES], trunk_ref[:, LANES:], proj_ref[...],
            jnp.where(inner, turned, sides[:part]).astype(jnp.bfloat16),
        ],
        0,
    )
    for peer in range(send_ref.shape[0]):
        send_ref[peer] = block


def features_kernel(got_ref, rows_ref, window_ref):
    peers, height, _ = got_ref.shape
    channels = 2 * height // 7
    part = channels // 2

    def take(first, count):
        return got_ref[:, first : first + count].reshape(peers * count, LANES)

    def project(bins, proj):
        return lax.dot_general(bins, proj, (((0,), (0,)), ((), ())), preferred_element_type=jnp.float32)

    proj = take(2 * channels, channels)
    sides = take(3 * channels, part)
    one = project(sides, take(2 * channels, part))
    two = project(sides, take(2 * channels + part, part))
    half = LANES // 2
    below = one[:8] + two[half : half + 8]
    above = one[LANES - 8 :] + two[half - 8 : half]
    row = lax.axis_index("row")
    far = jnp.where(lax.broadcasted_iota(jnp.int32, (8, 2 * CH), 1) >= CH, FAR, 0.0)
    above = jnp.where(row == 0, far, above)
    below = jnp.where(row == lax.axis_size("row") - 1, far, below)
    feat = jnp.concatenate(
        [above, project(take(0, channels), proj), project(take(channels, channels), proj), below], 0
    ).astype(jnp.bfloat16)
    rows_ref[...] = feat
    height = LANES + 16
    window_ref[...] = jnp.where(serves_odd(row, lax.axis_index("col")), feat[LANES:], feat[:height])


def weights_kernel(kernel_ref, gain_ref, bias_ref, weights_ref, twice_ref):
    twice_ref[...] = jnp.concatenate([bias_ref[...]] * 2, 1)
    weights_ref[...] = jnp.zeros_like(weights_ref)
    half_gain = 0.5 * gain_ref[...]
    for b in range(3):
        for a in range(3):
            total = kernel_ref[3 * a + b].astype(jnp.float32) + kernel_ref[3 * b + a].astype(jnp.float32)
            tap = (half_gain * total.T).astype(jnp.bfloat16)
            for place, out in enumerate(OUT_ORDER):
                first = (b * TAPS_IN + out + a) * CH
                weights_ref[first : first + CH, place * CH : (place + 1) * CH] = tap


def map_kernel(feat_ref, window_ref, weights_ref, bias_ref, out_ref, shift_ref, row_u, row_v, cols_ref, *rest, rows):
    acts, pairs, (stage_ref, sems) = rest[:RING], rest[RING : 2 * RING], rest[2 * RING :]
    step = pl.program_id(0)

    def positive(pair):
        return jnp.maximum(pair, jnp.zeros((), jnp.bfloat16))

    def generate(u_rows, v_rows, first, ring, place):
        for s in range(DIL):
            u = jnp.broadcast_to(u_rows[first + s : first + s + 1], (LANES, LANES))
            v = jnp.broadcast_to(v_rows[first + s : first + s + 1], (LANES, LANES))
            for b in range(3):
                pair = (u * cols_ref[b, 0] + (v + cols_ref[b, 1])).astype(jnp.bfloat16)
                if b == 1:
                    pairs[ring][place, s] = pair
                else:
                    acts[ring][b // 2, place, s] = positive(pair)

    def copies(group):
        return [
            pltpu.make_async_copy(
                stage_ref.at[pl.ds(STEP_ROWS * group + first, PIECE)],
                out_ref.at[pl.ds(STEP_ROWS * group + first, PIECE)],
                sems.at[group, first // PIECE],
            )
            for first in range(0, STEP_ROWS, PIECE)
        ]

    @pl.when(step == 0)
    def _():
        low = lax.broadcasted_iota(jnp.int32, (rows + 16, LANES), 1) < CH
        here = feat_ref[...].astype(jnp.float32)
        shift_ref[: rows + 16] = here
        ahead = shift_ref[DIL : DIL + rows + 16]
        row_u[: rows + 16] = jnp.where(low, here, pltpu.roll(ahead, CH, 1))
        row_v[: rows + 16] = jnp.where(low, pltpu.roll(here, CH, 1), ahead)
        window = window_ref[...].astype(jnp.float32)
        turned = pltpu.roll(window, CH, 1)
        height = LANES + 16
        for part, (left, right) in enumerate(((window, turned), (turned, window))):
            shift_ref[:height] = jnp.where(low[:height], left, right)
            for b in range(3):
                cols_ref[b, part] = shift_ref[4 + DIL * b : 4 + DIL * b + LANES]
        for chunk in range(3):
            base = 8 * chunk
            ring, place = ((RING - 1, 1), (0, 0), (0, 1))[chunk]
            generate(row_u[base : base + 8], row_v[base : base + 8], DIL, ring, place)

    low = lax.broadcasted_iota(jnp.int32, (LANES, LANES), 1) < CH
    bias = bias_ref[...]

    for which in range(RING):
        group = RING * step + which
        old = (which - 1) % RING
        first = pl.multiple_of(STEP_ROWS * group + 24, 8)
        u_rows = row_u[pl.ds(first, 16)]
        v_rows = row_v[pl.ds(first, 16)]
        for place in range(2):
            generate(u_rows, v_rows, 8 * place + DIL, (which + 1) % RING, place)
        taken = []
        for b in range(3):
            for ring, place in ((old, 1), (which, 0), (which, 1)):
                rows_in = positive(pairs[ring][place]) if b == 1 else acts[ring][b // 2, place]
                taken.append(rows_in.reshape(DIL * LANES, LANES))
        result = jnp.dot(jnp.concatenate(taken, 1), weights_ref[...], preferred_element_type=jnp.float32)
        for s in range(DIL):
            here = slice(s * LANES, (s + 1) * LANES)
            mixed = jnp.where(low, pairs[which][1, s].astype(jnp.float32), pairs[old][1, s].astype(jnp.float32))
            bases = (pairs[which][0, s].astype(jnp.float32), mixed)
            for side, base in enumerate(bases):
                value = base + result[here, side * LANES : (side + 1) * LANES] + bias
                flat = value.astype(out_ref.dtype).T
                for e in range(2):
                    row = STEP_ROWS * group + DIL * OUT_ORDER[2 * side + e] + s
                    stage_ref[row] = flat[e * CH : (e + 1) * CH]
        for copy in copies(group):
            copy.start()

    @pl.when(step == rows // (RING * STEP_ROWS) - 1)
    def _():
        for group in range(rows // STEP_ROWS):
            for copy in copies(group):
                copy.wait()


def local_map(feat, window, conv_kernel, norm_gain, norm_bias):
    rows = feat.shape[0] - 16
    depth = 3 * TAPS_IN * CH
    weights, bias = pl.pallas_call(
        weights_kernel,
        out_shape=[
            pltpu.VMEM((depth, GROUP * CH), jnp.bfloat16),
            pltpu.VMEM((1, 2 * CH), jnp.float32),
        ],
        name="weights",
    )(conv_kernel, norm_gain[None], norm_bias[None])

    whole = lambda shape: pl.BlockSpec(shape, lambda i: (0,) * len(shape))
    act = pltpu.VMEM((2, 2, DIL, LANES, LANES), jnp.bfloat16)
    pair = pltpu.VMEM((2, DIL, LANES, LANES), jnp.bfloat16)
    features = pltpu.VMEM((rows + 48, LANES), jnp.float32)
    return pl.pallas_call(
        lambda *refs: map_kernel(*refs, rows=rows),
        grid=(rows // (RING * STEP_ROWS),),
        in_specs=[whole(feat.shape), whole(window.shape), whole((depth, GROUP * CH)), whole((1, 2 * CH))],
        out_specs=pl.BlockSpec(memory_space=pl.ANY),
        out_shape=jax.ShapeDtypeStruct((rows, CH, LANES), jnp.bfloat16),
        scratch_shapes=[
            features, features, features, pltpu.VMEM((3, 2, LANES, LANES), jnp.float32),
            *[act] * RING, *[pair] * RING,
            pltpu.VMEM((rows, CH, LANES), jnp.bfloat16),
            pltpu.SemaphoreType.DMA((rows // STEP_ROWS, STEP_ROWS // PIECE)),
        ],
        compiler_params=pltpu.CompilerParams(
            dimension_semantics=("arbitrary",), vmem_limit_bytes=VMEM_BYTES
        ),
        name="pair_map",
    )(feat, window, weights, bias)


def hops(source, target):
    total = 0
    for size, place in (
        (4, lambda r, c: r // 2 % 4), (8, lambda r, c: c // 4), (8, lambda r, c: r // 8 * 4 + c % 4),
    ):
        apart = (place(*source) - place(*target)) % size
        total += min(apart, size - apart)
    return total


def pairing(sources, targets):
    for limit in range(16):
        owner = {}

        def settle(source, seen):
            for target in sorted(targets, key=lambda t: hops(source, t)):
                if target in seen or hops(source, target) > limit:
                    continue
                seen.add(target)
                if target not in owner or settle(owner[target], seen):
                    owner[target] = source
                    return True
            return False

        if all(settle(source, set()) for source in sources):
            return {source: target for target, source in owner.items()}
    raise ValueError("no pairing")


def serves_odd(row, col):
    inner = (col % 4 == 1) | (col % 4 == 2)
    return inner ^ (row % 2 == 1)


def window_routes(n_row, n_col):
    routes = []
    for r in range(n_row):
        for odd in range(2):
            sources = [(r, c) for c in range(n_col) if serves_odd(r, c) == odd]
            targets = [(t, 2 * r + odd) for t in range(n_row)]
            for (sr, sc), (tr, tc) in pairing(sources, targets).items():
                routes.append((sr * n_col + sc, tr * n_col + tc))
    return sorted(routes)


def in_vmem(array):
    return pltpu.with_memory_space_constraint(array, pltpu.VMEM)


def per_device(trunk, proj_weight, conv_kernel, norm_gain, norm_bias):
    rows, channels = trunk.shape
    n_row, n_col = lax.axis_size("row"), lax.axis_size("col")

    own = trunk.T
    one = lax.ppermute(own, "row", [(r, r ^ 1) for r in range(n_row)])
    two = lax.ppermute(own, "row", [(r, ((r + 1) ^ 1) - 1) for r in range(1, n_row - 1)])
    send = pl.pallas_call(
        pack_kernel,
        out_shape=pltpu.VMEM((n_col, 7 * channels // 2, LANES), jnp.bfloat16),
        name="pack",
    )(own, in_vmem(one), in_vmem(two), proj_weight)
    got = lax.all_to_all(send, "col", 0, 0, tiled=True)
    feat, window = pl.pallas_call(
        features_kernel,
        out_shape=[
            pltpu.VMEM((rows + 16, 2 * CH), jnp.bfloat16),
            pltpu.VMEM((LANES + 16, 2 * CH), jnp.bfloat16),
        ],
        name="features",
    )(in_vmem(got))
    window = lax.ppermute(window, ("row", "col"), window_routes(n_row, n_col))
    return local_map(feat, window, conv_kernel, norm_gain, norm_bias)


def solution(mesh):
    in_specs = (P("row", "col"), P("col", None), P(), P(), P())
    out_specs = P("row", None, "col")
    return jax.shard_map(
        per_device, mesh=mesh, in_specs=in_specs, out_specs=out_specs, check_vma=False
    )
```

```python
import jax
import jax.numpy as jnp
from jax import lax
from jax.experimental import pallas as pl
from jax.experimental.pallas import tpu as pltpu
from jax.sharding import PartitionSpec as P

DIL = 4
CH = 64
FAR = -1e30
GROUP = 4
STEP_ROWS = GROUP * DIL
LANES = 128
TAPS_IN = GROUP + 2
RING = 4
PIECE = 8
OUT_ORDER = (1, 2, 3, 0)
VMEM_BYTES = 48 << 20


def pack_kernel(trunk_ref, one_ref, two_ref, proj_ref, send_ref):
    channels, rows = trunk_ref.shape
    part = channels // 2
    lane = lax.broadcasted_iota(jnp.int32, (channels, LANES), 1)
    one_is_above = lax.axis_index("row") % 2 == 1

    def side(lanes, from_one):
        return jnp.where(from_one, one_ref[:, lanes], two_ref[:, lanes]).astype(jnp.float32)

    below = side(slice(0, LANES), ~one_is_above)
    above = side(slice(rows - LANES, rows), one_is_above)
    sides = jnp.where(lane < LANES // 2, below, above)
    turned = pltpu.roll(sides[part:], LANES // 2, 1)
    inner = (lane[:part] >= LANES // 4) & (lane[:part] < LANES - LANES // 4)
    block = jnp.concatenate(
        [
            trunk_ref[:, :LANES], trunk_ref[:, LANES:], proj_ref[...],
            jnp.where(inner, turned, sides[:part]).astype(jnp.bfloat16),
        ],
        0,
    )
    for peer in range(send_ref.shape[0]):
        send_ref[peer] = block


def features_kernel(got_ref, rows_ref, window_ref):
    peers, height, _ = got_ref.shape
    channels = 2 * height // 7
    part = channels // 2

    def take(first, count):
        return got_ref[:, first : first + count].reshape(peers * count, LANES)

    def project(bins, proj):
        return lax.dot_general(bins, proj, (((0,), (0,)), ((), ())), preferred_element_type=jnp.float32)

    proj = take(2 * channels, channels)
    sides = take(3 * channels, part)
    one = project(sides, take(2 * channels, part))
    two = project(sides, take(2 * channels + part, part))
    half = LANES // 2
    below = one[:8] + two[half : half + 8]
    above = one[LANES - 8 :] + two[half - 8 : half]
    row = lax.axis_index("row")
    far = jnp.where(lax.broadcasted_iota(jnp.int32, (8, 2 * CH), 1) >= CH, FAR, 0.0)
    above = jnp.where(row == 0, far, above)
    below = jnp.where(row == lax.axis_size("row") - 1, far, below)
    feat = jnp.concatenate(
        [above, project(take(0, channels), proj), project(take(channels, channels), proj), below], 0
    ).astype(jnp.bfloat16)
    rows_ref[...] = feat
    height = LANES + 16
    window_ref[...] = jnp.where(serves_odd(row, lax.axis_index("col")), feat[LANES:], feat[:height])


def prepare_kernel(kernel_ref, gain_ref, bias_ref, feat_ref, weights_ref, twice_ref, row_u, row_v, shift_ref):
    count = feat_ref.shape[0]
    low = lax.broadcasted_iota(jnp.int32, (count, LANES), 1) < CH
    here = feat_ref[...].astype(jnp.float32)
    shift_ref[:count] = here
    shift_ref[count:] = jnp.zeros_like(shift_ref[count:])
    ahead = shift_ref[DIL : DIL + count]
    for ref, value in (
        (row_u, jnp.where(low, here, pltpu.roll(ahead, CH, 1))),
        (row_v, jnp.where(low, pltpu.roll(here, CH, 1), ahead)),
    ):
        ref[:count] = value
        ref[count:] = jnp.zeros_like(ref[count:])
    twice_ref[...] = jnp.concatenate([bias_ref[...]] * 2, 1)
    weights_ref[...] = jnp.zeros_like(weights_ref)
    half_gain = 0.5 * gain_ref[...]
    for b in range(3):
        for a in range(3):
            total = kernel_ref[3 * a + b].astype(jnp.float32) + kernel_ref[3 * b + a].astype(jnp.float32)
            tap = (half_gain * total.T).astype(jnp.bfloat16)
            for place, out in enumerate(OUT_ORDER):
                first = (b * TAPS_IN + out + a) * CH
                weights_ref[first : first + CH, place * CH : (place + 1) * CH] = tap


def map_kernel(row_u, row_v, window_ref, weights_ref, bias_ref, out_ref, shift_ref, cols_ref, short_ref, *rest, rows):
    acts, pairs, (stage_ref, sems) = rest[:RING], rest[RING : 2 * RING], rest[2 * RING :]
    step = pl.program_id(0)

    def positive(pair):
        return jnp.maximum(pair, jnp.zeros((), jnp.bfloat16))

    def generate(u_rows, v_rows, first, ring, place):
        for s in range(DIL):
            u = jnp.broadcast_to(u_rows[first + s : first + s + 1], (16, LANES))
            v = jnp.broadcast_to(v_rows[first + s : first + s + 1], (16, LANES))
            u, v, short_u, short_v = (
                jnp.broadcast_to(x[None], (LANES // 16, 16, LANES)).reshape(LANES, LANES)
                for x in (u, v, u.astype(jnp.bfloat16), v.astype(jnp.bfloat16))
            )
            pairs[ring][place, s] = (u * cols_ref[1, 0] + (v + cols_ref[1, 1])).astype(jnp.bfloat16)
            for side in range(2):
                near = short_u * short_ref[side, 0] + (short_v + short_ref[side, 1])
                acts[ring][side, place, s] = positive(near)

    def copies(group):
        return [
            pltpu.make_async_copy(
                stage_ref.at[pl.ds(STEP_ROWS * group + first, PIECE)],
                out_ref.at[pl.ds(STEP_ROWS * group + first, PIECE)],
                sems.at[group, first // PIECE],
            )
            for first in range(0, STEP_ROWS, PIECE)
        ]

    @pl.when(step == 0)
    def _():
        low = lax.broadcasted_iota(jnp.int32, (LANES + 16, LANES), 1) < CH
        window = window_ref[...].astype(jnp.float32)
        turned = pltpu.roll(window, CH, 1)
        for part, (left, right) in enumerate(((window, turned), (turned, window))):
            shift_ref[...] = jnp.where(low, left, right)
            for b in range(3):
                cols_ref[b, part] = shift_ref[4 + DIL * b : 4 + DIL * b + LANES]
            for side in range(2):
                short_ref[side, part] = cols_ref[2 * side, part].astype(jnp.bfloat16)
        for chunk in range(3):
            base = 8 * chunk
            ring, place = ((RING - 1, 1), (0, 0), (0, 1))[chunk]
            generate(row_u[base : base + 8], row_v[base : base + 8], DIL, ring, place)

    low = lax.broadcasted_iota(jnp.int32, (LANES, LANES), 1) < CH
    bias = bias_ref[...]

    for which in range(RING):
        group = RING * step + which
        old = (which - 1) % RING
        first = pl.multiple_of(STEP_ROWS * group + 24, 8)
        u_rows = row_u[pl.ds(first, 16)]
        v_rows = row_v[pl.ds(first, 16)]
        for place in range(2):
            generate(u_rows, v_rows, 8 * place + DIL, (which + 1) % RING, place)
        taken = []
        for b in range(3):
            for ring, place in ((old, 1), (which, 0), (which, 1)):
                rows_in = positive(pairs[ring][place]) if b == 1 else acts[ring][b // 2, place]
                taken.append(rows_in.reshape(DIL * LANES, LANES))
        result = jnp.dot(jnp.concatenate(taken, 1), weights_ref[...], preferred_element_type=jnp.float32)
        for s in range(DIL):
            here = slice(s * LANES, (s + 1) * LANES)
            mixed = jnp.where(low, pairs[which][1, s].astype(jnp.float32), pairs[old][1, s].astype(jnp.float32))
            bases = (pairs[which][0, s].astype(jnp.float32), mixed)
            for side, base in enumerate(bases):
                value = base + result[here, side * LANES : (side + 1) * LANES] + bias
                flat = value.astype(out_ref.dtype).T
                for e in range(2):
                    row = STEP_ROWS * group + DIL * OUT_ORDER[2 * side + e] + s
                    stage_ref[row] = flat[e * CH : (e + 1) * CH]
        for copy in copies(group):
            copy.start()

    @pl.when(step == rows // (RING * STEP_ROWS) - 1)
    def _():
        for group in range(rows // STEP_ROWS):
            for copy in copies(group):
                copy.wait()


def local_map(feat, window, conv_kernel, norm_gain, norm_bias):
    rows = feat.shape[0] - 16
    depth = 3 * TAPS_IN * CH
    row_part = pltpu.VMEM((rows + 48, LANES), jnp.float32)
    weights, bias, row_u, row_v = pl.pallas_call(
        prepare_kernel,
        out_shape=[
            pltpu.VMEM((depth, GROUP * CH), jnp.bfloat16), pltpu.VMEM((1, 2 * CH), jnp.float32), row_part, row_part,
        ],
        scratch_shapes=[pltpu.VMEM((rows + 32, LANES), jnp.float32)],
        name="prepare",
    )(conv_kernel, norm_gain[None], norm_bias[None], feat)

    whole = lambda shape: pl.BlockSpec(shape, lambda i: (0,) * len(shape))
    act = pltpu.VMEM((2, 2, DIL, LANES, LANES), jnp.bfloat16)
    pair = pltpu.VMEM((2, DIL, LANES, LANES), jnp.bfloat16)
    return pl.pallas_call(
        lambda *refs: map_kernel(*refs, rows=rows),
        grid=(rows // (RING * STEP_ROWS),),
        in_specs=[whole(a.shape) for a in (row_u, row_v, window, weights, bias)],
        out_specs=pl.BlockSpec(memory_space=pl.ANY),
        out_shape=jax.ShapeDtypeStruct((rows, CH, LANES), jnp.bfloat16),
        scratch_shapes=[
            pltpu.VMEM((LANES + 16, LANES), jnp.float32), pltpu.VMEM((3, 2, LANES, LANES), jnp.float32),
            pltpu.VMEM((2, 2, LANES, LANES), jnp.bfloat16),
            *[act] * RING, *[pair] * RING,
            pltpu.VMEM((rows, CH, LANES), jnp.bfloat16),
            pltpu.SemaphoreType.DMA((rows // STEP_ROWS, STEP_ROWS // PIECE)),
        ],
        compiler_params=pltpu.CompilerParams(
            dimension_semantics=("arbitrary",), vmem_limit_bytes=VMEM_BYTES
        ),
        name="pair_map",
    )(row_u, row_v, window, weights, bias)


def hops(source, target):
    total = 0
    for size, place in (
        (4, lambda r, c: r // 2 % 4), (8, lambda r, c: c // 4), (8, lambda r, c: r // 8 * 4 + c % 4),
    ):
        apart = (place(*source) - place(*target)) % size
        total += min(apart, size - apart)
    return total


def pairing(sources, targets):
    for limit in range(16):
        owner = {}

        def settle(source, seen):
            for target in sorted(targets, key=lambda t: hops(source, t)):
                if target in seen or hops(source, target) > limit:
                    continue
                seen.add(target)
                if target not in owner or settle(owner[target], seen):
                    owner[target] = source
                    return True
            return False

        if all(settle(source, set()) for source in sources):
            return {source: target for target, source in owner.items()}
    raise ValueError("no pairing")


def serves_odd(row, col):
    inner = (col % 4 == 1) | (col % 4 == 2)
    return inner ^ (row % 2 == 1)


def window_routes(n_row, n_col):
    routes = []
    for r in range(n_row):
        for odd in range(2):
            sources = [(r, c) for c in range(n_col) if serves_odd(r, c) == odd]
            targets = [(t, 2 * r + odd) for t in range(n_row)]
            for (sr, sc), (tr, tc) in pairing(sources, targets).items():
                routes.append((sr * n_col + sc, tr * n_col + tc))
    return sorted(routes)


def in_vmem(array):
    return pltpu.with_memory_space_constraint(array, pltpu.VMEM)


def per_device(trunk, proj_weight, conv_kernel, norm_gain, norm_bias):
    rows, channels = trunk.shape
    n_row, n_col = lax.axis_size("row"), lax.axis_size("col")

    own = trunk.T
    one = lax.ppermute(own, "row", [(r, r ^ 1) for r in range(n_row)])
    two = lax.ppermute(own, "row", [(r, ((r + 1) ^ 1) - 1) for r in range(1, n_row - 1)])
    send = pl.pallas_call(
        pack_kernel,
        out_shape=pltpu.VMEM((n_col, 7 * channels // 2, LANES), jnp.bfloat16),
        name="pack",
    )(own, in_vmem(one), in_vmem(two), proj_weight)
    got = lax.all_to_all(send, "col", 0, 0, tiled=True)
    feat, window = pl.pallas_call(
        features_kernel,
        out_shape=[
            pltpu.VMEM((rows + 16, 2 * CH), jnp.bfloat16),
            pltpu.VMEM((LANES + 16, 2 * CH), jnp.bfloat16),
        ],
        name="features",
    )(in_vmem(got))
    window = lax.ppermute(window, ("row", "col"), window_routes(n_row, n_col))
    return local_map(feat, window, conv_kernel, norm_gain, norm_bias)


def solution(mesh):
    in_specs = (P("row", "col"), P("col", None), P(), P(), P())
    out_specs = P("row", None, "col")
    return jax.shard_map(
        per_device, mesh=mesh, in_specs=in_specs, out_specs=out_specs, check_vma=False
    )
```

```python
import jax
import jax.numpy as jnp
from jax import lax
from jax.experimental import pallas as pl
from jax.experimental.pallas import tpu as pltpu
from jax.sharding import PartitionSpec as P

DIL = 4
CH = 64
FAR = -1e30
GROUP = 4
STEP_ROWS = GROUP * DIL
LANES = 128
TAPS_IN = GROUP + 2
RING = 8
PIECE = 8
OUT_ORDER = (1, 2, 3, 0)
VMEM_BYTES = 48 << 20


def pack_kernel(trunk_ref, one_ref, two_ref, proj_ref, send_ref):
    channels, rows = trunk_ref.shape
    part = channels // 2
    lane = lax.broadcasted_iota(jnp.int32, (channels, LANES), 1)
    one_is_above = lax.axis_index("row") % 2 == 1

    def side(lanes, from_one):
        return jnp.where(from_one, one_ref[:, lanes], two_ref[:, lanes]).astype(jnp.float32)

    below = side(slice(0, LANES), ~one_is_above)
    above = side(slice(rows - LANES, rows), one_is_above)
    sides = jnp.where(lane < LANES // 2, below, above)
    turned = pltpu.roll(sides[part:], LANES // 2, 1)
    inner = (lane[:part] >= LANES // 4) & (lane[:part] < LANES - LANES // 4)
    block = jnp.concatenate(
        [
            trunk_ref[:, :LANES], trunk_ref[:, LANES:], proj_ref[...],
            jnp.where(inner, turned, sides[:part]).astype(jnp.bfloat16),
        ],
        0,
    )
    for peer in range(send_ref.shape[0]):
        send_ref[peer] = block


def features_kernel(got_ref, rows_ref, window_ref):
    peers, height, _ = got_ref.shape
    channels = 2 * height // 7
    part = channels // 2

    def take(first, count):
        return got_ref[:, first : first + count].reshape(peers * count, LANES)

    def project(bins, proj):
        return lax.dot_general(bins, proj, (((0,), (0,)), ((), ())), preferred_element_type=jnp.float32)

    proj = take(2 * channels, channels)
    sides = take(3 * channels, part)
    one = project(sides, take(2 * channels, part))
    two = project(sides, take(2 * channels + part, part))
    half = LANES // 2
    below = one[:8] + two[half : half + 8]
    above = one[LANES - 8 :] + two[half - 8 : half]
    row = lax.axis_index("row")
    far = jnp.where(lax.broadcasted_iota(jnp.int32, (8, 2 * CH), 1) >= CH, FAR, 0.0)
    above = jnp.where(row == 0, far, above)
    below = jnp.where(row == lax.axis_size("row") - 1, far, below)
    feat = jnp.concatenate(
        [above, project(take(0, channels), proj), project(take(channels, channels), proj), below], 0
    ).astype(jnp.bfloat16)
    rows_ref[...] = feat
    height = LANES + 16
    window_ref[...] = jnp.where(serves_odd(row, lax.axis_index("col")), feat[LANES:], feat[:height])


def prepare_kernel(kernel_ref, gain_ref, bias_ref, feat_ref, weights_ref, twice_ref, row_u, row_v, shift_ref):
    count = feat_ref.shape[0]
    low = lax.broadcasted_iota(jnp.int32, (count, LANES), 1) < CH
    here = feat_ref[...].astype(jnp.float32)
    shift_ref[:count] = here
    shift_ref[count:] = jnp.zeros_like(shift_ref[count:])
    ahead = shift_ref[DIL : DIL + count]
    for ref, value in (
        (row_u, jnp.where(low, here, pltpu.roll(ahead, CH, 1))),
        (row_v, jnp.where(low, pltpu.roll(here, CH, 1), ahead)),
    ):
        ref[:count] = value
        ref[count:] = jnp.zeros_like(ref[count:])
    twice_ref[...] = jnp.concatenate([bias_ref[...]] * 2, 1)
    weights_ref[...] = jnp.zeros_like(weights_ref)
    half_gain = 0.5 * gain_ref[...]
    for b in range(3):
        for a in range(3):
            total = kernel_ref[3 * a + b].astype(jnp.float32) + kernel_ref[3 * b + a].astype(jnp.float32)
            tap = (half_gain * total.T).astype(jnp.bfloat16)
            for place, out in enumerate(OUT_ORDER):
                first = (b * TAPS_IN + out + a) * CH
                weights_ref[first : first + CH, place * CH : (place + 1) * CH] = tap


def map_kernel(row_u, row_v, window_ref, weights_ref, bias_ref, out_ref, shift_ref, cols_ref, short_ref, *rest, rows):
    acts, pairs, (stage_ref, sems) = rest[:RING], rest[RING : 2 * RING], rest[2 * RING :]
    step = pl.program_id(0)

    def positive(pair):
        return jnp.maximum(pair, jnp.zeros((), jnp.bfloat16))

    def generate(u_rows, v_rows, first, ring, place):
        for s in range(DIL):
            u = jnp.broadcast_to(u_rows[first + s : first + s + 1], (16, LANES))
            v = jnp.broadcast_to(v_rows[first + s : first + s + 1], (16, LANES))
            u, v, short_u, short_v = (
                jnp.broadcast_to(x[None], (LANES // 16, 16, LANES)).reshape(LANES, LANES)
                for x in (u, v, u.astype(jnp.bfloat16), v.astype(jnp.bfloat16))
            )
            pairs[ring][place, s] = (u * cols_ref[1, 0] + (v + cols_ref[1, 1])).astype(jnp.bfloat16)
            for side in range(2):
                near = short_u * short_ref[side, 0] + (short_v + short_ref[side, 1])
                acts[ring][side, place, s] = positive(near)

    def copies(group):
        return [
            pltpu.make_async_copy(
                stage_ref.at[pl.ds(STEP_ROWS * group + first, PIECE)],
                out_ref.at[pl.ds(STEP_ROWS * group + first, PIECE)],
                sems.at[group, first // PIECE],
            )
            for first in range(0, STEP_ROWS, PIECE)
        ]

    @pl.when(step == 0)
    def _():
        low = lax.broadcasted_iota(jnp.int32, (LANES + 16, LANES), 1) < CH
        window = window_ref[...].astype(jnp.float32)
        turned = pltpu.roll(window, CH, 1)
        for part, (left, right) in enumerate(((window, turned), (turned, window))):
            shift_ref[...] = jnp.where(low, left, right)
            for b in range(3):
                cols_ref[b, part] = shift_ref[4 + DIL * b : 4 + DIL * b + LANES]
            for side in range(2):
                short_ref[side, part] = cols_ref[2 * side, part].astype(jnp.bfloat16)
        for chunk in range(3):
            base = 8 * chunk
            ring, place = ((RING - 1, 1), (0, 0), (0, 1))[chunk]
            generate(row_u[base : base + 8], row_v[base : base + 8], DIL, ring, place)

    low = lax.broadcasted_iota(jnp.int32, (LANES, LANES), 1) < CH
    bias = bias_ref[...]

    for which in range(RING):
        group = RING * step + which
        old = (which - 1) % RING
        first = pl.multiple_of(STEP_ROWS * group + 24, 8)
        u_rows = row_u[pl.ds(first, 16)]
        v_rows = row_v[pl.ds(first, 16)]
        for place in range(2):
            generate(u_rows, v_rows, 8 * place + DIL, (which + 1) % RING, place)
        taken = []
        for b in range(3):
            for ring, place in ((old, 1), (which, 0), (which, 1)):
                rows_in = positive(pairs[ring][place]) if b == 1 else acts[ring][b // 2, place]
                taken.append(rows_in.reshape(DIL * LANES, LANES))
        result = jnp.dot(jnp.concatenate(taken, 1), weights_ref[...], preferred_element_type=jnp.float32)
        for s in range(DIL):
            here = slice(s * LANES, (s + 1) * LANES)
            mixed = jnp.where(low, pairs[which][1, s].astype(jnp.float32), pairs[old][1, s].astype(jnp.float32))
            bases = (pairs[which][0, s].astype(jnp.float32), mixed)
            for side, base in enumerate(bases):
                value = base + result[here, side * LANES : (side + 1) * LANES] + bias
                flat = value.astype(out_ref.dtype).T
                for e in range(2):
                    row = STEP_ROWS * group + DIL * OUT_ORDER[2 * side + e] + s
                    stage_ref[row] = flat[e * CH : (e + 1) * CH]
        for copy in copies(group):
            copy.start()

    @pl.when(step == rows // (RING * STEP_ROWS) - 1)
    def _():
        for group in range(rows // STEP_ROWS):
            for copy in copies(group):
                copy.wait()


def local_map(feat, window, conv_kernel, norm_gain, norm_bias):
    rows = feat.shape[0] - 16
    depth = 3 * TAPS_IN * CH
    row_part = pltpu.VMEM((rows + 48, LANES), jnp.float32)
    weights, bias, row_u, row_v = pl.pallas_call(
        prepare_kernel,
        out_shape=[
            pltpu.VMEM((depth, GROUP * CH), jnp.bfloat16), pltpu.VMEM((1, 2 * CH), jnp.float32), row_part, row_part,
        ],
        scratch_shapes=[pltpu.VMEM((rows + 32, LANES), jnp.float32)],
        name="prepare",
    )(conv_kernel, norm_gain[None], norm_bias[None], feat)

    whole = lambda shape: pl.BlockSpec(shape, lambda i: (0,) * len(shape))
    act = pltpu.VMEM((2, 2, DIL, LANES, LANES), jnp.bfloat16)
    pair = pltpu.VMEM((2, DIL, LANES, LANES), jnp.bfloat16)
    return pl.pallas_call(
        lambda *refs: map_kernel(*refs, rows=rows),
        grid=(rows // (RING * STEP_ROWS),),
        in_specs=[whole(a.shape) for a in (row_u, row_v, window, weights, bias)],
        out_specs=pl.BlockSpec(memory_space=pl.ANY),
        out_shape=jax.ShapeDtypeStruct((rows, CH, LANES), jnp.bfloat16),
        scratch_shapes=[
            pltpu.VMEM((LANES + 16, LANES), jnp.float32), pltpu.VMEM((3, 2, LANES, LANES), jnp.float32),
            pltpu.VMEM((2, 2, LANES, LANES), jnp.bfloat16),
            *[act] * RING, *[pair] * RING,
            pltpu.VMEM((rows, CH, LANES), jnp.bfloat16),
            pltpu.SemaphoreType.DMA((rows // STEP_ROWS, STEP_ROWS // PIECE)),
        ],
        compiler_params=pltpu.CompilerParams(
            dimension_semantics=("arbitrary",), vmem_limit_bytes=VMEM_BYTES
        ),
        name="pair_map",
    )(row_u, row_v, window, weights, bias)


def hops(source, target):
    total = 0
    for size, place in (
        (4, lambda r, c: r // 2 % 4), (8, lambda r, c: c // 4), (8, lambda r, c: r // 8 * 4 + c % 4),
    ):
        apart = (place(*source) - place(*target)) % size
        total += min(apart, size - apart)
    return total


def pairing(sources, targets):
    for limit in range(16):
        owner = {}

        def settle(source, seen):
            for target in sorted(targets, key=lambda t: hops(source, t)):
                if target in seen or hops(source, target) > limit:
                    continue
                seen.add(target)
                if target not in owner or settle(owner[target], seen):
                    owner[target] = source
                    return True
            return False

        if all(settle(source, set()) for source in sources):
            return {source: target for target, source in owner.items()}
    raise ValueError("no pairing")


def serves_odd(row, col):
    inner = (col % 4 == 1) | (col % 4 == 2)
    return inner ^ (row % 2 == 1)


def window_routes(n_row, n_col):
    routes = []
    for r in range(n_row):
        for odd in range(2):
            sources = [(r, c) for c in range(n_col) if serves_odd(r, c) == odd]
            targets = [(t, 2 * r + odd) for t in range(n_row)]
            for (sr, sc), (tr, tc) in pairing(sources, targets).items():
                routes.append((sr * n_col + sc, tr * n_col + tc))
    return sorted(routes)


def in_vmem(array):
    return pltpu.with_memory_space_constraint(array, pltpu.VMEM)


def per_device(trunk, proj_weight, conv_kernel, norm_gain, norm_bias):
    rows, channels = trunk.shape
    n_row, n_col = lax.axis_size("row"), lax.axis_size("col")

    own = trunk.T
    one = lax.ppermute(own, "row", [(r, r ^ 1) for r in range(n_row)])
    two = lax.ppermute(own, "row", [(r, ((r + 1) ^ 1) - 1) for r in range(1, n_row - 1)])
    send = pl.pallas_call(
        pack_kernel,
        out_shape=pltpu.VMEM((n_col, 7 * channels // 2, LANES), jnp.bfloat16),
        name="pack",
    )(own, in_vmem(one), in_vmem(two), proj_weight)
    got = lax.all_to_all(send, "col", 0, 0, tiled=True)
    feat, window = pl.pallas_call(
        features_kernel,
        out_shape=[
            pltpu.VMEM((rows + 16, 2 * CH), jnp.bfloat16),
            pltpu.VMEM((LANES + 16, 2 * CH), jnp.bfloat16),
        ],
        name="features",
    )(in_vmem(got))
    window = lax.ppermute(window, ("row", "col"), window_routes(n_row, n_col))
    return local_map(feat, window, conv_kernel, norm_gain, norm_bias)


def solution(mesh):
    in_specs = (P("row", "col"), P("col", None), P(), P(), P())
    out_specs = P("row", None, "col")
    return jax.shard_map(
        per_device, mesh=mesh, in_specs=in_specs, out_specs=out_specs, check_vma=False
    )
```
